128 devices in a mesh: grp: 2 (over core), dev: 64 (over z, x, y).
Axes of the slice: x: 4, y: 4, z: 4, core: 2. Of those that a mesh axis runs over, the one named last changes fastest.
Arguments:
- tokens: bfloat16 [32768, 2048], P(('grp', 'dev')), may hold values from -6 to 6
- modulation: float32 [128, 12288], P(('grp', 'dev')), may hold values from -3 to 3
- w_query: bfloat16 [2048, 1024], P(('grp', 'dev')), may hold values from -1 to 1
- w_key: bfloat16 [2048, 1024], P(('grp', 'dev')), may hold values from -1 to 1
- w_value: bfloat16 [2048, 1024], P(('grp', 'dev')), may hold values from -0.125 to 0.125
- w_out: bfloat16 [1024, 2048], P(None, ('grp', 'dev')), may hold values from -0.1875 to 0.1875
- w_in: bfloat16 [64, 2048, 4096], P('dev', None, 'grp'), may hold values from -0.125 to 0.125
- w_back: bfloat16 [64, 4096, 2048], P('dev', 'grp'), may hold values from -0.09375 to 0.09375
- routes: int32 [32768, 2], P(('grp', 'dev')), may hold values from 0 to 63, all different within a row; in each aligned block of 256 rows (0 to 255, 256 to 511, ...) at most 10 rows name the same one
- route_prob: float32 [32768, 2], P(('grp', 'dev')), may hold values from 0.2 to 1
Outputs:
- block_out: bfloat16 [32768, 2048], P(('grp', 'dev'))
The draws below stay inside these ranges and needn't reach their ends.
Inputs may be any that keep to these rules, and one draw needn't show every extreme that they name: `routes`: the 2 experts of a token differ. Among the 256 tokens of one device (aligned blocks of rows), no expert is named more than 10 times, a bound that some block reaches.
All inputs are finite; a program needn't handle non-finite values.
Results may differ from the reference program's by a relative error of at most 0.0055.
Values may be sent and summed in bfloat16 or wider, within the bound.
No kernel may reach another device: no remote copies, remote signals or barrier semaphores. Data moves between devices by JAX's collectives and lax.ppermute only.
A program may use at most 128 MiB of HBM per device.

```python
import math
import jax
import jax.numpy as jnp
import numpy as np
from jax import lax

D = 2048
HEADS = 8
HDIM = 128
HW = 1024
HID = 4096
TOP = 2
E = 64
SEQ = 256
TOK_DEV = 256
IMAGES = 128
TOKENS = 32768
CAP = 10
N_GRP = 2
N_DEV = 64


def paired_query(key):
    base_rows = jnp.clip(jax.random.normal(jax.random.fold_in(key, 101), (D, HW), jnp.float32), -4.0, 4.0) * D ** (-0.5)
    noise_rows = jnp.clip(jax.random.normal(jax.random.fold_in(key, 202), (D, HW), jnp.float32), -4.0, 4.0) * D ** (-0.5)
    query_part = base_rows
    key_part = noise_rows
    return (jnp.clip(query_part, -1.0, 1.0), jnp.clip(key_part, -1.0, 1.0))


def draw_w_query(key, part):
    return paired_query(key)[0].astype(jnp.bfloat16)


def draw_w_key(key, part):
    return paired_query(key)[1].astype(jnp.bfloat16)


def level_of(key, dims, pieces, least, largest):
    loudness = 1.0
    for axis_at, shards_of in pieces:
        steps = jax.random.uniform(jax.random.fold_in(jax.random.fold_in(key, 6), axis_at), (shards_of,), jnp.float32, least / len(pieces), largest / len(pieces))
        loudness = loudness * jnp.repeat(jnp.exp(steps), dims[axis_at] // shards_of).reshape((-1,) + (1,) * (len(dims) - 1 - axis_at))
    return loudness


def shared_out(own_key, own, number, rows, amount, top, limit, skew):
    order = jax.random.permutation(own_key, amount)
    packed, common = shares(amount, rows * top, limit, skew, True), shares(amount, rows * top, limit, skew, False)
    places = jnp.arange(amount)

    def named(sizes, offset_by):
        used = int((sizes > 0).sum())
        fixed = max(1, used // 4)
        moved = fixed + (places - fixed + offset_by * (used - fixed)) % max(1, amount - fixed)
        return jnp.zeros((amount,), jnp.int32).at[order[jnp.where(places < fixed, places, moved)]].set(jnp.asarray(sizes, jnp.int32))

    sizes = jnp.where(number % 4 == 0, named(packed, number // 4), named(common, number - number // 4 - 1))
    mixed = jax.random.permutation(jax.random.fold_in(own, 3), amount)
    donor, taker = mixed[0:amount // 2 * 2:2], mixed[1:amount // 2 * 2:2]
    room = jnp.minimum(sizes[donor] - 1, limit - sizes[taker]) // 2
    room = jnp.where((donor == order[0]) | (taker == order[0]) | (sizes[taker] == 0), 0, jnp.maximum(room, 0))
    moved = jax.random.randint(jax.random.fold_in(own, 4), (amount // 2,), 0, 1 << 20) % (room + 1)
    sizes = sizes.at[donor].add(-moved).at[taker].add(moved)
    members = jnp.searchsorted(jnp.cumsum(sizes), jnp.arange(rows * top), side="right").astype(jnp.int32)
    table = members.reshape(top, rows).T
    table = table[jax.random.permutation(jax.random.fold_in(own, 1), rows)]
    offset_by = jax.random.randint(jax.random.fold_in(own, 2), (rows, 1), 0, top)
    return jnp.take_along_axis(table, (jnp.arange(top)[None, :] + offset_by) % top, axis=1)


def shares(count, total, most, skew, full):
    portions = [(1 << 20) // math.isqrt(rank ** skew) + 1 for rank in range(1, count + 1)]
    largest = most if full else min(most, max(-(-total // count), total * portions[0] // sum(portions)))
    least = 1 if total - largest >= count - 1 else 0
    given, rest = [largest] + [least] * (count - 1), total - largest - least * (count - 1)
    while rest > 0:
        free = [i for i in range(1, count) if given[i] < largest] or [i for i in range(1, count) if given[i] < most]
        pool, left = sum([portions[i] for i in free]), rest
        for i in free:
            addition = min(most - given[i], max(1, left * portions[i] // pool), rest)
            given[i] = given[i] + addition
            rest = rest - addition
    return np.array(given)


def noise(own_key, shape, scale, most, cuts=(), kind=jnp.bfloat16):
    loudness = level_of(own_key, shape, cuts, -0.22, 0.18) if cuts else 1.0
    drawn = jax.random.normal(own_key, shape, jnp.float32) * scale * loudness
    return jnp.minimum(jnp.maximum(drawn, -most), most).astype(kind)


def setup_inputs(seed: int = 0) -> dict:
    keys = jax.random.split(jax.random.key(seed), 11)
    tokens = noise(keys[0], (TOKENS, D), 1.0, 6.0, ((0, 128),))
    modulation = noise(keys[1], (IMAGES, 6 * D), 0.5, 3.0, ((0, 128),), jnp.float32)
    w_query = draw_w_query(jax.random.fold_in(keys[10], 71), 0)
    w_key = draw_w_key(jax.random.fold_in(keys[10], 71), 0)
    w_value = noise(keys[4], (D, HW), D ** -0.5, 0.125, ((0, 128),))
    w_out = noise(keys[5], (HW, D), HW ** -0.5, 0.1875, ((1, 128),))
    w_in = noise(keys[6], (E, D, HID), D ** -0.5, 0.125, ((0, 64), (2, 2)))
    w_back = noise(keys[7], (E, HID, D), HID ** -0.5, 0.09375, ((0, 64), (1, 2)))
    routes_keys = jax.random.split(jax.random.fold_in(keys[8], 1), TOKENS // TOK_DEV)
    routes_turns = jax.random.permutation(jax.random.fold_in(keys[8], 3), TOKENS // TOK_DEV)
    routes = jax.vmap(lambda own, number: shared_out(jax.random.fold_in(keys[8], 2), own, number, TOK_DEV, E, TOP, CAP, 2))(routes_keys, routes_turns).reshape((TOKENS, TOP))
    route_prob = jnp.clip(0.2 + 0.8 * jax.random.uniform(keys[9], (TOKENS, TOP), jnp.float32) ** level_of(keys[9], (TOKENS, TOP), ((0, 128),), -0.2, 0.2), 0.2, 1.0)
    return dict(tokens=tokens, modulation=modulation, w_query=w_query, w_key=w_key, w_value=w_value, w_out=w_out, w_in=w_in, w_back=w_back, routes=routes, route_prob=route_prob)


def normalize(values):
    row_mean = lax.optimization_barrier(jnp.mean(values, axis=-1, keepdims=True))
    centered = values - row_mean
    variance = lax.optimization_barrier(jnp.mean(centered * centered, axis=-1, keepdims=True))
    return centered * lax.rsqrt(variance + 1e-06)

def slot_table(choice_ids):
    onehot = (choice_ids[:, None] == jnp.arange(E, dtype=jnp.int32)[None, :]).astype(jnp.int32)
    before = jnp.cumsum(onehot, axis=0) - onehot
    return (choice_ids * CAP + lax.optimization_barrier(jnp.sum(before * onehot, axis=1))).astype(jnp.int32)

def reference(tokens, modulation, w_query, w_key, w_value, w_out, w_in, w_back, routes, route_prob):
    devices = N_GRP * N_DEV
    mod_terms = modulation.reshape(IMAGES, 6, 1, D)
    residual = tokens.astype(jnp.float32).reshape(IMAGES, SEQ, D)
    normed_one = (normalize(residual) * (1.0 + mod_terms[:, 1]) + mod_terms[:, 0]).astype(jnp.bfloat16).reshape(TOKENS, D)
    query_rows = jnp.dot(normed_one, w_query, preferred_element_type=jnp.float32).astype(jnp.bfloat16)
    key_rows = jnp.dot(normed_one, w_key, preferred_element_type=jnp.float32).astype(jnp.bfloat16)
    value_rows = jnp.dot(normed_one, w_value, preferred_element_type=jnp.float32).astype(jnp.bfloat16)
    query_four = query_rows.astype(jnp.float32).reshape(IMAGES, SEQ, HEADS, HDIM)
    key_four = key_rows.astype(jnp.float32).reshape(IMAGES, SEQ, HEADS, HDIM)
    value_four = value_rows.astype(jnp.float32).reshape(IMAGES, SEQ, HEADS, HDIM)
    scores = jnp.einsum('bqhd,bkhd->bhqk', query_four, key_four) * HDIM ** (-0.5)
    row_peak = lax.optimization_barrier(jnp.max(scores, axis=-1, keepdims=True))
    exponent = jnp.exp(scores - row_peak)
    attn_weights = (exponent / lax.optimization_barrier(jnp.sum(exponent, axis=-1, keepdims=True))).astype(jnp.bfloat16)
    mixed_heads = jnp.einsum('bhqk,bkhd->bqhd', attn_weights.astype(jnp.float32), value_four)
    mixed_heads = mixed_heads.astype(jnp.bfloat16).reshape(TOKENS, HW)
    projected = jnp.dot(mixed_heads, w_out, preferred_element_type=jnp.float32).reshape(IMAGES, SEQ, D)
    after_attn = residual + mod_terms[:, 2] * projected
    normed_two = (normalize(after_attn) * (1.0 + mod_terms[:, 4]) + mod_terms[:, 3]).astype(jnp.bfloat16)
    normed_two = normed_two.reshape(devices, TOK_DEV, D)
    slots = jax.vmap(slot_table)(routes.reshape(devices, TOK_DEV * TOP))
    token_of = jnp.arange(TOK_DEV * TOP, dtype=jnp.int32) // TOP

    def fill_slots(source_rows, where):
        return jnp.zeros((E * CAP, D), jnp.bfloat16).at[where].set(source_rows[token_of])
    buffers = jax.vmap(fill_slots)(normed_two, slots)
    per_expert = buffers.reshape(devices, E, CAP, D).transpose(1, 0, 2, 3).reshape(E, devices * CAP, D)

    def expert_pass(operands):
        expert_rows, w_first, w_second = operands
        hidden = jax.nn.gelu(jnp.dot(expert_rows, w_first, preferred_element_type=jnp.float32), approximate=True)
        hidden = hidden.astype(jnp.bfloat16)
        return jnp.dot(hidden, w_second, preferred_element_type=jnp.float32).astype(jnp.bfloat16)
    outputs = lax.map(expert_pass, (per_expert, w_in, w_back))
    returned = outputs.reshape(E, devices, CAP, D).transpose(1, 0, 2, 3).reshape(devices, E * CAP, D)
    picked = jax.vmap(lambda table, where: table[where])(returned, slots)
    picked = picked.astype(jnp.float32).reshape(TOKENS, TOP, D)
    expert_mix = lax.optimization_barrier(jnp.sum(route_prob[:, :, None] * picked, axis=1)).reshape(IMAGES, SEQ, D)
    return (after_attn + mod_terms[:, 5] * expert_mix).astype(jnp.bfloat16).reshape(TOKENS, D)
```

```python
import functools

import jax
import jax.numpy as jnp
from jax import lax
from jax.experimental import pallas as pl
from jax.experimental.pallas import tpu as pltpu
from jax.sharding import PartitionSpec as P

HEADS = 8
HDIM = 128
TOP = 2
CAP = 10
PAIRS = (5,)
BF16 = jnp.bfloat16
F32 = jnp.float32
VMEM_LIMIT = 58 * 1024 * 1024


def mm(a, b):
    return jnp.dot(a, b, preferred_element_type=F32)


def normalize(values):
    row_mean = jnp.mean(values, axis=-1, keepdims=True)
    centered = values - row_mean
    variance = jnp.mean(centered * centered, axis=-1, keepdims=True)
    return centered * lax.rsqrt(variance + 1e-06)


def fold_matrix(transposed):
    row = lax.broadcasted_iota(jnp.int32, (256, 256), 1 if transposed else 0)
    col = lax.broadcasted_iota(jnp.int32, (256, 256), 0 if transposed else 1)
    source = ((row // 2) % 4) * 64 + (row // 8) * 2 + row % 2
    return (source == col).astype(BF16)


def fold(rows, matrix):
    stacked = jnp.concatenate([rows[:, q * 512 : (q + 1) * 512] for q in range(4)], axis=0)
    return mm(matrix, stacked).astype(BF16)


def attention_kernel(pairs, xn, tok, mod, sel, wq, wk, wv, wo, after, *rest):
    sends, mixed = rest[:-1], rest[-1]
    step = pl.program_id(0)

    @pl.when(step < 4)
    def _():
        x = xn[...]
        q = mm(x, wq[...]).astype(BF16)
        k = mm(x, wk[...]).astype(BF16)
        v = mm(x, wv[...]).astype(BF16)
        outs = []
        for h in range(2):
            cut = slice(h * HDIM, (h + 1) * HDIM)
            scores = lax.dot_general(
                q[:, cut], k[:, cut], (((1,), (1,)), ((), ())), preferred_element_type=F32
            ) * HDIM ** (-0.5)
            exponent = jnp.exp(scores - jnp.max(scores, axis=-1, keepdims=True))
            weights = (exponent / jnp.sum(exponent, axis=-1, keepdims=True)).astype(BF16)
            outs.append(mm(weights, v[:, cut]).astype(BF16))
        mixed[:, pl.ds(pl.multiple_of(step * 256, 256), 256)] = jnp.concatenate(outs, axis=1)

    @pl.when(step >= 4)
    def _():
        at = pl.ds(pl.multiple_of((step - 4) * 512, 512), 512)
        projected = lax.dot_general(
            mixed[...], wo[...], (((1,), (1,)), ((), ())), preferred_element_type=F32
        )
        after[:, at] = tok[:, at].astype(F32) + mod[2:3, at] * projected

    @pl.when(step == 7)
    def _():
        normed = (normalize(after[...]) * (1.0 + mod[4:5, :]) + mod[3:4, :]).astype(BF16)
        matrix = fold_matrix(False)
        pair = 0
        for count, send in zip(pairs, sends):
            for j in range(count):
                rows = mm(sel[pair * 128 : (pair + 1) * 128, :], normed).astype(BF16)
                for g in range(2):
                    send[g * 256 : (g + 1) * 256, j * 512 : (j + 1) * 512] = fold(
                        rows[g * 64 : (g + 1) * 64, :], matrix
                    )
                pair += 1


def attention(pairs, xn, tok, mod, sel, weights):
    rows, width = xn.shape
    whole = lambda a: pl.BlockSpec(a.shape, lambda i: (0,) * a.ndim)
    part = lambda first: pl.BlockSpec((width, 256), lambda i: (0, first + jnp.minimum(i, 3)))
    shapes = [jax.ShapeDtypeStruct((rows, width), F32)]
    shapes += [jax.ShapeDtypeStruct((512, 512 * n), BF16) for n in pairs]
    return pl.pallas_call(
        functools.partial(attention_kernel, pairs),
        grid=(8,),
        in_specs=[
            whole(xn),
            whole(tok),
            whole(mod),
            whole(sel),
            part(0),
            part(4),
            part(8),
            pl.BlockSpec((512, 1024), lambda i: (jnp.maximum(i - 4, 0), 3)),
        ],
        out_specs=[whole(s) for s in shapes],
        out_shape=shapes,
        scratch_shapes=[pltpu.VMEM((rows, 1024), BF16)],
        compiler_params=pltpu.CompilerParams(vmem_limit_bytes=VMEM_LIMIT),
        cost_estimate=pl.CostEstimate(
            flops=7 * 10**9, transcendentals=10**6, bytes_accessed=24 * 10**6
        ),
        name="attention",
    )(xn, tok, mod, sel, weights, weights, weights, weights)


def expert_kernel(pairs, own, other, w_first, w_second, own_out, other_out, x, hidden, out):
    step = pl.program_id(0)
    blocks = [(src, j) for src in range(2) for j in range(pairs)]

    @pl.when(step == 0)
    def _():
        matrix = fold_matrix(True)
        for n, (src, j) in enumerate(blocks):
            ref = (own, other)[src]
            for g in range(2):
                flat = mm(matrix, ref[g * 256 : (g + 1) * 256, j * 512 : (j + 1) * 512]).astype(BF16)
                for q in range(4):
                    x[n * 128 + g * 64 : n * 128 + (g + 1) * 64, q * 512 : (q + 1) * 512] = flat[
                        q * 64 : (q + 1) * 64, :
                    ]

    @pl.when(step < 8)
    def _():
        at = pl.ds(pl.multiple_of(step * 256, 256), 256)
        product = mm(x[...], w_first[...])
        hidden[:, at] = jax.nn.gelu(product, approximate=True).astype(BF16)

    @pl.when(step >= 8)
    def _():
        at = pl.ds(pl.multiple_of((step - 8) * 256, 256), 256)
        out[:, at] = mm(hidden[...], w_second[...]).astype(BF16)

    @pl.when(step == 15)
    def _():
        matrix = fold_matrix(False)
        for n, (src, j) in enumerate(blocks):
            ref = (own_out, other_out)[src]
            for g in range(2):
                ref[g * 256 : (g + 1) * 256, j * 512 : (j + 1) * 512] = fold(
                    out[n * 128 + g * 64 : n * 128 + (g + 1) * 64, :], matrix
                )


def expert_half(pairs, own, other, w_first, w_second):
    width, half = w_first.shape
    rows = 256 * pairs
    whole = pl.BlockSpec(own.shape, lambda i: (0, 0))
    return pl.pallas_call(
        functools.partial(expert_kernel, pairs),
        grid=(16,),
        in_specs=[
            whole,
            whole,
            pl.BlockSpec((width, 256), lambda i: (0, jnp.minimum(i, 7))),
            pl.BlockSpec((half, 256), lambda i: (0, jnp.maximum(i - 8, 0))),
        ],
        out_specs=[whole, whole],
        out_shape=[jax.ShapeDtypeStruct(own.shape, BF16)] * 2,
        scratch_shapes=[
            pltpu.VMEM((rows, width), BF16),
            pltpu.VMEM((rows, half), BF16),
            pltpu.VMEM((rows, width), BF16),
        ],
        compiler_params=pltpu.CompilerParams(vmem_limit_bytes=VMEM_LIMIT),
        cost_estimate=pl.CostEstimate(
            flops=4 * rows * width * half,
            transcendentals=rows * half,
            bytes_accessed=4 * width * half + 8 * rows * width,
        ),
        name="experts",
    )(own, other, w_first, w_second)


def combine_kernel(pairs, after, mod, pick0, pick1, prob, *rest):
    backs, result, flat = rest[: len(pairs)], rest[-2], rest[-1]
    matrix = fold_matrix(True)
    pair = 0
    for count, back in zip(pairs, backs):
        for j in range(count):
            for g in range(2):
                rows = mm(matrix, back[g * 256 : (g + 1) * 256, j * 512 : (j + 1) * 512]).astype(BF16)
                for q in range(4):
                    top = pair * 128 + g * 64
                    flat[top : top + 64, q * 512 : (q + 1) * 512] = rows[q * 64 : (q + 1) * 64, :]
            pair += 1
    for q in range(4):
        cut = slice(q * 512, (q + 1) * 512)
        mix = prob[:, 0:1] * mm(pick0[...], flat[:, cut]) + prob[:, 1:2] * mm(pick1[...], flat[:, cut])
        result[:, cut] = (after[:, cut] + mod[5:6, cut] * mix).astype(BF16)


def combine(pairs, after, mod, pick0, pick1, prob, backs):
    rows, width = after.shape
    vmem = pl.BlockSpec(memory_space=pltpu.VMEM)
    return pl.pallas_call(
        functools.partial(combine_kernel, pairs),
        in_specs=[vmem] * (5 + len(backs)),
        out_specs=vmem,
        out_shape=jax.ShapeDtypeStruct((rows, width), BF16),
        scratch_shapes=[pltpu.VMEM((128 * sum(pairs), width), BF16)],
        compiler_params=pltpu.CompilerParams(vmem_limit_bytes=VMEM_LIMIT),
        cost_estimate=pl.CostEstimate(
            flops=3 * 10**9, transcendentals=0, bytes_accessed=7 * 10**6
        ),
        name="combine",
    )(after, mod, pick0, pick1, prob, *backs)


def slots_of(routes, experts):
    tokens = routes.shape[0]
    ids = jnp.arange(experts, dtype=jnp.int32)
    chosen = [(routes[:, k : k + 1] == ids[None, :]) for k in range(TOP)]
    taken = sum(c.astype(BF16) for c in chosen)
    order = jnp.arange(tokens, dtype=jnp.int32)
    earlier = (order[:, None] > order[None, :]).astype(BF16)
    before = mm(earlier, taken)
    slots = []
    for k in range(TOP):
        rank = jnp.sum(jnp.where(chosen[k], before, 0.0), axis=1).astype(jnp.int32)
        slots.append((rank // 2) * (2 * experts) + routes[:, k] * 2 + rank % 2)
    return slots


def body(tokens, modulation, w_query, w_key, w_value, w_out, w_in, w_back, routes, route_prob):
    tok_rows, width = tokens.shape
    mod = modulation.reshape(6, width)
    pieces = jnp.concatenate([w_query, w_key, w_value, w_out.T], axis=1)
    weights = lax.all_gather(pieces, ("grp", "dev"), axis=0, tiled=True)

    xn = (normalize(tokens.astype(F32)) * (1.0 + mod[1:2]) + mod[0:1]).astype(BF16)
    experts = lax.axis_size("dev")
    rows = experts * CAP
    slots = slots_of(routes, experts)
    ids = jnp.arange(rows, dtype=jnp.int32)
    sel = sum((ids[:, None] == s[None, :]).astype(BF16) for s in slots)
    picks = [(s[:, None] == ids[None, :]).astype(BF16) for s in slots]

    after, *sends = attention(PAIRS, xn, tokens, mod, sel, weights)
    swap = [(0, 1), (1, 0)]
    backs = []
    for count, send in zip(PAIRS, sends):
        send = send.reshape(experts, 8, 512 * count)
        own = lax.all_to_all(send, "dev", split_axis=0, concat_axis=0, tiled=True)
        own = own.reshape(512, 512 * count)
        other = lax.ppermute(own, "grp", swap)
        own_out, other_out = expert_half(count, own, other, w_in[0], w_back[0])
        arrived = lax.ppermute(other_out, "grp", swap)
        total = (own_out.astype(F32) + arrived.astype(F32)).astype(BF16)
        total = total.reshape(experts, 8, 512 * count)
        back = lax.all_to_all(total, "dev", split_axis=0, concat_axis=0, tiled=True)
        backs.append(back.reshape(512, 512 * count))
    return combine(PAIRS, after, mod, picks[0], picks[1], route_prob, backs)


def solution(mesh):
    in_specs = (
        P(("grp", "dev"), None),
        P(("grp", "dev"), None),
        P(("grp", "dev"), None),
        P(("grp", "dev"), None),
        P(("grp", "dev"), None),
        P(None, ("grp", "dev")),
        P("dev", None, "grp"),
        P("dev", "grp", None),
        P(("grp", "dev"), None),
        P(("grp", "dev"), None),
    )
    out_specs = P(("grp", "dev"), None)
    return jax.shard_map(body, mesh=mesh, in_specs=in_specs, out_specs=out_specs, check_vma=False)
```

```python
import jax
import jax.numpy as jnp
from jax import lax
from jax.experimental import pallas as pl
from jax.experimental.pallas import tpu as pltpu
from jax.sharding import PartitionSpec as P

HEADS = 8
HDIM = 128
TOP = 2
CAP = 10
PAIRS = (3, 2)
TILE = 512
WIDE = 1024
TALL = 2048
MB = 256
BF16 = jnp.bfloat16
F32 = jnp.float32
MIB = 1024 * 1024


def mm(a, b):
    return jnp.dot(a, b, preferred_element_type=F32)


def in_hbm(array):
    return pltpu.with_memory_space_constraint(array, pltpu.HBM)


def normalize(values):
    row_mean = jnp.mean(values, axis=-1, keepdims=True)
    centered = values - row_mean
    variance = jnp.mean(centered * centered, axis=-1, keepdims=True)
    return centered * lax.rsqrt(variance + 1e-06)


def fold_matrix(transposed):
    row = lax.broadcasted_iota(jnp.int32, (256, 256), 1 if transposed else 0)
    col = lax.broadcasted_iota(jnp.int32, (256, 256), 0 if transposed else 1)
    source = ((row // 2) % 4) * 64 + (row // 8) * 2 + row % 2
    return (source == col).astype(BF16)


def fold(rows, matrix):
    stacked = jnp.concatenate([rows[:, q * 512 : (q + 1) * 512] for q in range(4)], axis=0)
    return mm(matrix, stacked).astype(BF16)


def attention_kernel(xn, tok, mod, sel, weights, after_out, *rest):
    sends, (after, mixed, held, sems) = rest[: len(PAIRS)], rest[len(PAIRS) :]
    width, inner = xn.shape[1], mixed.shape[1]
    groups = inner // WIDE
    copies = []

    def fetch(rows, cols):
        copies.append(
            pltpu.make_async_copy(weights.at[rows, cols], held.at[rows, cols], sems.at[len(copies)])
        )
        copies[-1].start()

    for n in range(groups):
        for part in range(3):
            fetch(pl.ds(0, width), pl.ds(part * inner + n * WIDE, WIDE))
    for n in range(width // TALL):
        fetch(pl.ds(n * TALL, TALL), pl.ds(3 * inner, inner))

    for n in range(groups):
        projections = []
        for part in range(3):
            copies[3 * n + part].wait()
            first = part * inner + n * WIDE
            projections.append(mm(xn[...], held[:, first : first + WIDE]).astype(BF16))
        q, k, v = projections
        for h in range(WIDE // HDIM):
            cut = slice(h * HDIM, (h + 1) * HDIM)
            scores = lax.dot_general(
                q[:, cut], k[:, cut], (((1,), (1,)), ((), ())), preferred_element_type=F32
            ) * HDIM ** (-0.5)
            exponent = jnp.exp(scores - jnp.max(scores, axis=-1, keepdims=True))
            attn = (exponent / jnp.sum(exponent, axis=-1, keepdims=True)).astype(BF16)
            mixed[:, n * WIDE + h * HDIM : n * WIDE + (h + 1) * HDIM] = mm(attn, v[:, cut]).astype(BF16)

    for n in range(width // TALL):
        copies[3 * groups + n].wait()
        cut = slice(n * TALL, (n + 1) * TALL)
        projected = lax.dot_general(
            mixed[...], held[cut, 3 * inner :], (((1,), (1,)), ((), ())), preferred_element_type=F32
        )
        after[:, cut] = tok[:, cut].astype(F32) + mod[2:3, cut] * projected

    keep = pltpu.make_async_copy(after, after_out, sems.at[len(copies)])
    keep.start()
    normed = (normalize(after[...]) * (1.0 + mod[4:5, :]) + mod[3:4, :]).astype(BF16)
    matrix = fold_matrix(False)
    pair = 0
    for send in sends:
        for j in range(send.shape[1] // 512):
            rows = mm(sel[pair * 128 : (pair + 1) * 128, :], normed).astype(BF16)
            for g in range(2):
                send[g * 256 : (g + 1) * 256, j * 512 : (j + 1) * 512] = fold(
                    rows[g * 64 : (g + 1) * 64, :], matrix
                )
            pair += 1
    keep.wait()


def attention(xn, tok, mod, sel, weights):
    rows, width = xn.shape
    inner = HEADS * HDIM
    vmem = pl.BlockSpec(memory_space=pltpu.VMEM)
    return pl.pallas_call(
        attention_kernel,
        in_specs=[vmem] * 4 + [pl.BlockSpec(memory_space=pltpu.HBM)],
        out_specs=[pl.BlockSpec(memory_space=pltpu.HBM)] + [vmem] * len(PAIRS),
        out_shape=[pltpu.HBM((rows, width), F32)]
        + [jax.ShapeDtypeStruct((512, 512 * n), BF16) for n in PAIRS],
        scratch_shapes=[
            pltpu.VMEM((rows, width), F32),
            pltpu.VMEM((rows, inner), BF16),
            pltpu.VMEM((width, 4 * inner), BF16),
            pltpu.SemaphoreType.DMA((3 * (inner // WIDE) + width // TALL + 1,)),
        ],
        compiler_params=pltpu.CompilerParams(vmem_limit_bytes=48 * MIB),
        cost_estimate=pl.CostEstimate(
            flops=7 * 10**9, transcendentals=10**6, bytes_accessed=24 * 10**6
        ),
        name="attention",
    )(xn, tok, mod, sel, in_hbm(weights))


def expert_kernel(own, other, w_first, w_second, own_out, other_out, x, hidden, first, second, sems):
    pairs = own.shape[1] // 512
    tiles = first.shape[1] // TILE
    blocks = [(src, j) for src in range(2) for j in range(pairs)]

    def fetch(which, n):
        source, target = ((w_first, first), (w_second, second))[which]
        cut = pl.ds(pl.multiple_of(n * TILE, TILE), TILE)
        return pltpu.make_async_copy(
            source.at[:, cut], target.at[:, cut], sems.at[which * tiles + n]
        )

    for which in range(2):
        for n in range(tiles):
            fetch(which, n).start()

    matrix = fold_matrix(True)
    for n, (src, j) in enumerate(blocks):
        ref = (own, other)[src]
        for g in range(2):
            flat = mm(matrix, ref[g * 256 : (g + 1) * 256, j * 512 : (j + 1) * 512]).astype(BF16)
            for q in range(4):
                x[n * 128 + g * 64 : n * 128 + (g + 1) * 64, q * 512 : (q + 1) * 512] = flat[
                    q * 64 : (q + 1) * 64, :
                ]

    @pl.loop(0, tiles)
    def _(n):
        fetch(0, n).wait()
        cut = pl.ds(pl.multiple_of(n * TILE, TILE), TILE)
        for m in range(0, x.shape[0], MB):
            product = mm(x[m : m + MB, :], first[:, cut])
            hidden[m : m + MB, cut] = jax.nn.gelu(product, approximate=True).astype(BF16)

    @pl.loop(0, tiles)
    def _(n):
        fetch(1, n).wait()
        cut = pl.ds(pl.multiple_of(n * TILE, TILE), TILE)
        for m in range(0, x.shape[0], MB):
            x[m : m + MB, cut] = mm(hidden[m : m + MB, :], second[:, cut]).astype(BF16)

    matrix = fold_matrix(False)
    for n, (src, j) in enumerate(blocks):
        ref = (own_out, other_out)[src]
        for g in range(2):
            ref[g * 256 : (g + 1) * 256, j * 512 : (j + 1) * 512] = fold(
                x[n * 128 + g * 64 : n * 128 + (g + 1) * 64, :], matrix
            )


def expert_half(own, other, w_first, w_second):
    width, half = w_first.shape
    rows = own.shape[1] // 2
    vmem = pl.BlockSpec(memory_space=pltpu.VMEM)
    hbm = pl.BlockSpec(memory_space=pltpu.HBM)
    return pl.pallas_call(
        expert_kernel,
        in_specs=[vmem, vmem, hbm, hbm],
        out_specs=[vmem, vmem],
        out_shape=[jax.ShapeDtypeStruct(own.shape, BF16)] * 2,
        scratch_shapes=[
            pltpu.VMEM((rows, width), BF16),
            pltpu.VMEM((rows, half), BF16),
            pltpu.VMEM((width, half), BF16),
            pltpu.VMEM((half, width), BF16),
            pltpu.SemaphoreType.DMA((2 * (half // TILE),)),
        ],
        compiler_params=pltpu.CompilerParams(vmem_limit_bytes=36 * MIB),
        cost_estimate=pl.CostEstimate(
            flops=4 * rows * width * half,
            transcendentals=rows * half,
            bytes_accessed=4 * width * half + 8 * rows * width,
        ),
        name="experts",
    )(own, other, in_hbm(w_first), in_hbm(w_second))


def combine_kernel(after_out, mod, pick0, pick1, prob, *rest):
    backs, (result, after, flat, sem) = rest[: len(PAIRS)], rest[len(PAIRS) :]
    kept = pltpu.make_async_copy(after_out, after, sem)
    kept.start()
    matrix = fold_matrix(True)
    top = 0
    for back in backs:
        for j in range(back.shape[1] // 512):
            for g in range(2):
                rows = mm(matrix, back[g * 256 : (g + 1) * 256, j * 512 : (j + 1) * 512]).astype(BF16)
                for q in range(4):
                    flat[top : top + 64, q * 512 : (q + 1) * 512] = rows[q * 64 : (q + 1) * 64, :]
                top += 64
    kept.wait()
    for q in range(4):
        cut = slice(q * 512, (q + 1) * 512)
        mix = prob[:, 0:1] * mm(pick0[...], flat[:, cut]) + prob[:, 1:2] * mm(pick1[...], flat[:, cut])
        result[:, cut] = (after[:, cut] + mod[5:6, cut] * mix).astype(BF16)


def combine(after, mod, pick0, pick1, prob, backs):
    rows, width = after.shape
    vmem = pl.BlockSpec(memory_space=pltpu.VMEM)
    return pl.pallas_call(
        combine_kernel,
        in_specs=[pl.BlockSpec(memory_space=pltpu.HBM)] + [vmem] * (4 + len(backs)),
        out_specs=vmem,
        out_shape=jax.ShapeDtypeStruct((rows, width), BF16),
        scratch_shapes=[
            pltpu.VMEM((rows, width), F32),
            pltpu.VMEM((128 * sum(PAIRS), width), BF16),
            pltpu.SemaphoreType.DMA,
        ],
        compiler_params=pltpu.CompilerParams(vmem_limit_bytes=16 * MIB),
        cost_estimate=pl.CostEstimate(
            flops=3 * 10**9, transcendentals=0, bytes_accessed=7 * 10**6
        ),
        name="combine",
    )(in_hbm(after), mod, pick0, pick1, prob, *backs)


def diagonal_order(experts):
    return sorted(range(experts), key=diagonal_place)


def diagonal_place(chip):
    z, x, y = chip // 16, (chip // 4) % 4, chip % 4
    return (y - z) % 4 * 16 + (x - z) % 4 * 4 + z


def slots_of(routes, experts):
    tokens = routes.shape[0]
    routes = diagonal_place(routes)
    ids = jnp.arange(experts, dtype=jnp.int32)
    chosen = [(routes[:, k : k + 1] == ids[None, :]) for k in range(TOP)]
    taken = sum(c.astype(BF16) for c in chosen)
    order = jnp.arange(tokens, dtype=jnp.int32)
    earlier = (order[:, None] > order[None, :]).astype(BF16)
    before = mm(earlier, taken)
    slots = []
    for k in range(TOP):
        rank = jnp.sum(jnp.where(chosen[k], before, 0.0), axis=1).astype(jnp.int32)
        slots.append((rank // 2) * (2 * experts) + routes[:, k] * 2 + rank % 2)
    return slots


def body(tokens, modulation, w_query, w_key, w_value, w_out, w_in, w_back, routes, route_prob):
    tok_rows, width = tokens.shape
    mod = modulation.reshape(6, width)
    pieces = jnp.concatenate([w_query, w_key, w_value, w_out.T], axis=1)
    weights = lax.all_gather(pieces, ("grp", "dev"), axis=0, tiled=True)

    xn = (normalize(tokens.astype(F32)) * (1.0 + mod[1:2]) + mod[0:1]).astype(BF16)
    experts = lax.axis_size("dev")
    rows = experts * CAP
    slots = slots_of(routes, experts)
    ids = jnp.arange(rows, dtype=jnp.int32)
    sel = sum((ids[:, None] == s[None, :]).astype(BF16) for s in slots)
    picks = [(s[:, None] == ids[None, :]).astype(BF16) for s in slots]

    after, *sends = attention(xn, tokens, mod, sel, weights)
    swap = [(0, 1), (1, 0)]

    def shuffle(rows):
        folded = rows.reshape(experts, 8, -1)
        groups = [diagonal_order(experts)]
        return lax.all_to_all(
            folded, "dev", split_axis=0, concat_axis=0, tiled=True, axis_index_groups=groups
        ).reshape(rows.shape)

    add = lambda a, b: (a.astype(F32) + b.astype(F32)).astype(BF16)
    w_first, w_second = w_in[0], w_back[0]

    own_a, own_b = [shuffle(send) for send in sends]
    mine_a, theirs_a = expert_half(own_a, lax.ppermute(own_a, "grp", swap), w_first, w_second)
    own_b, theirs_a = lax.optimization_barrier((own_b, theirs_a))
    other_b = lax.ppermute(own_b, "grp", swap)
    total_a = add(mine_a, lax.ppermute(theirs_a, "grp", swap))
    total_a, other_b = lax.optimization_barrier((total_a, other_b))
    back_a = shuffle(total_a)
    mine_b, theirs_b = expert_half(own_b, other_b, w_first, w_second)
    back_a, theirs_b = lax.optimization_barrier((back_a, theirs_b))
    total_b = add(mine_b, lax.ppermute(theirs_b, "grp", swap))
    backs = [back_a, shuffle(total_b)]
    return combine(after, mod, picks[0], picks[1], route_prob, backs)


def solution(mesh):
    in_specs = (
        P(("grp", "dev"), None),
        P(("grp", "dev"), None),
        P(("grp", "dev"), None),
        P(("grp", "dev"), None),
        P(("grp", "dev"), None),
        P(None, ("grp", "dev")),
        P("dev", None, "grp"),
        P("dev", "grp", None),
        P(("grp", "dev"), None),
        P(("grp", "dev"), None),
    )
    out_specs = P(("grp", "dev"), None)
    return jax.shard_map(body, mesh=mesh, in_specs=in_specs, out_specs=out_specs, check_vma=False)
```

```python
import jax
import jax.numpy as jnp
from jax import lax
from jax.experimental import pallas as pl
from jax.experimental.pallas import tpu as pltpu
from jax.sharding import PartitionSpec as P

HEADS = 8
HDIM = 128
TOP = 2
CAP = 10
PAIRS = (2, 3)
TILE = 512
WIDE = 1024
TALL = 2048
MB = 256
BF16 = jnp.bfloat16
F32 = jnp.float32
MIB = 1024 * 1024


def mm(a, b):
    return jnp.dot(a, b, preferred_element_type=F32)


def in_hbm(array):
    return pltpu.with_memory_space_constraint(array, pltpu.HBM)


def normalize(values):
    row_mean = jnp.mean(values, axis=-1, keepdims=True)
    centered = values - row_mean
    variance = jnp.mean(centered * centered, axis=-1, keepdims=True)
    return centered * lax.rsqrt(variance + 1e-06)


def fold_matrix(transposed):
    row = lax.broadcasted_iota(jnp.int32, (256, 256), 1 if transposed else 0)
    col = lax.broadcasted_iota(jnp.int32, (256, 256), 0 if transposed else 1)
    source = ((row // 2) % 4) * 64 + (row // 8) * 2 + row % 2
    return (source == col).astype(BF16)


def fold(rows, matrix):
    stacked = jnp.concatenate([rows[:, q * 512 : (q + 1) * 512] for q in range(4)], axis=0)
    return mm(matrix, stacked).astype(BF16)


def attention_kernel(xn, tok, mod, sel, weights, after_out, *rest):
    sends, (after, mixed, held, sems) = rest[: len(PAIRS)], rest[len(PAIRS) :]
    width, inner = xn.shape[1], mixed.shape[1]
    groups = inner // WIDE
    copies = []

    def fetch(rows, cols):
        copies.append(
            pltpu.make_async_copy(weights.at[rows, cols], held.at[rows, cols], sems.at[len(copies)])
        )
        copies[-1].start()

    for n in range(groups):
        for part in range(3):
            fetch(pl.ds(0, width), pl.ds(part * inner + n * WIDE, WIDE))
    for n in range(width // TALL):
        fetch(pl.ds(n * TALL, TALL), pl.ds(3 * inner, inner))

    for n in range(groups):
        projections = []
        for part in range(3):
            copies[3 * n + part].wait()
            first = part * inner + n * WIDE
            projections.append(mm(xn[...], held[:, first : first + WIDE]).astype(BF16))
        q, k, v = projections
        for h in range(WIDE // HDIM):
            cut = slice(h * HDIM, (h + 1) * HDIM)
            scores = lax.dot_general(
                q[:, cut], k[:, cut], (((1,), (1,)), ((), ())), preferred_element_type=F32
            ) * HDIM ** (-0.5)
            exponent = jnp.exp(scores - jnp.max(scores, axis=-1, keepdims=True))
            attn = (exponent / jnp.sum(exponent, axis=-1, keepdims=True)).astype(BF16)
            mixed[:, n * WIDE + h * HDIM : n * WIDE + (h + 1) * HDIM] = mm(attn, v[:, cut]).astype(BF16)

    for n in range(width // TALL):
        copies[3 * groups + n].wait()
        cut = slice(n * TALL, (n + 1) * TALL)
        projected = lax.dot_general(
            mixed[...], held[cut, 3 * inner :], (((1,), (1,)), ((), ())), preferred_element_type=F32
        )
        after[:, cut] = tok[:, cut].astype(F32) + mod[2:3, cut] * projected

    keep = pltpu.make_async_copy(after, after_out, sems.at[len(copies)])
    keep.start()
    normed = (normalize(after[...]) * (1.0 + mod[4:5, :]) + mod[3:4, :]).astype(BF16)
    matrix = fold_matrix(False)
    pair = 0
    for send in sends:
        for j in range(send.shape[1] // 512):
            rows = mm(sel[pair * 128 : (pair + 1) * 128, :], normed).astype(BF16)
            for g in range(2):
                send[g * 256 : (g + 1) * 256, j * 512 : (j + 1) * 512] = fold(
                    rows[g * 64 : (g + 1) * 64, :], matrix
                )
            pair += 1
    keep.wait()


def attention(xn, tok, mod, sel, weights):
    rows, width = xn.shape
    inner = HEADS * HDIM
    vmem = pl.BlockSpec(memory_space=pltpu.VMEM)
    return pl.pallas_call(
        attention_kernel,
        in_specs=[vmem] * 4 + [pl.BlockSpec(memory_space=pltpu.HBM)],
        out_specs=[pl.BlockSpec(memory_space=pltpu.HBM)] + [vmem] * len(PAIRS),
        out_shape=[pltpu.HBM((rows, width), F32)]
        + [jax.ShapeDtypeStruct((512, 512 * n), BF16) for n in PAIRS],
        scratch_shapes=[
            pltpu.VMEM((rows, width), F32),
            pltpu.VMEM((rows, inner), BF16),
            pltpu.VMEM((width, 4 * inner), BF16),
            pltpu.SemaphoreType.DMA((3 * (inner // WIDE) + width // TALL + 1,)),
        ],
        compiler_params=pltpu.CompilerParams(vmem_limit_bytes=26 * MIB),
        cost_estimate=pl.CostEstimate(
            flops=7 * 10**9, transcendentals=10**6, bytes_accessed=24 * 10**6
        ),
        name="attention",
    )(xn, tok, mod, sel, in_hbm(weights))


def expert_kernel(own, other, w_first, w_second, own_out, other_out, x, hidden, first, second, sems):
    pairs = own.shape[1] // 512
    tiles = first.shape[1] // TILE
    blocks = [(src, j) for src in range(2) for j in range(pairs)]

    def fetch(which, n):
        source, target = ((w_first, first), (w_second, second))[which]
        cut = pl.ds(pl.multiple_of(n * TILE, TILE), TILE)
        return pltpu.make_async_copy(
            source.at[:, cut], target.at[:, cut], sems.at[which * tiles + n]
        )

    for which in range(2):
        for n in range(tiles):
            fetch(which, n).start()

    matrix = fold_matrix(True)
    for n, (src, j) in enumerate(blocks):
        ref = (own, other)[src]
        for g in range(2):
            flat = mm(matrix, ref[g * 256 : (g + 1) * 256, j * 512 : (j + 1) * 512]).astype(BF16)
            for q in range(4):
                x[n * 128 + g * 64 : n * 128 + (g + 1) * 64, q * 512 : (q + 1) * 512] = flat[
                    q * 64 : (q + 1) * 64, :
                ]

    @pl.loop(0, tiles)
    def _(n):
        fetch(0, n).wait()
        cut = pl.ds(pl.multiple_of(n * TILE, TILE), TILE)
        for m in range(0, x.shape[0], MB):
            product = mm(x[m : m + MB, :], first[:, cut])
            hidden[m : m + MB, cut] = jax.nn.gelu(product, approximate=True).astype(BF16)

    @pl.loop(0, tiles)
    def _(n):
        fetch(1, n).wait()
        cut = pl.ds(pl.multiple_of(n * TILE, TILE), TILE)
        for m in range(0, x.shape[0], MB):
            x[m : m + MB, cut] = mm(hidden[m : m + MB, :], second[:, cut]).astype(BF16)

    matrix = fold_matrix(False)
    for n, (src, j) in enumerate(blocks):
        ref = (own_out, other_out)[src]
        for g in range(2):
            ref[g * 256 : (g + 1) * 256, j * 512 : (j + 1) * 512] = fold(
                x[n * 128 + g * 64 : n * 128 + (g + 1) * 64, :], matrix
            )


def expert_half(own, other, w_first, w_second):
    width, half = w_first.shape
    rows = own.shape[1] // 2
    vmem = pl.BlockSpec(memory_space=pltpu.VMEM)
    hbm = pl.BlockSpec(memory_space=pltpu.HBM)
    return pl.pallas_call(
        expert_kernel,
        in_specs=[vmem, vmem, hbm, hbm],
        out_specs=[vmem, vmem],
        out_shape=[jax.ShapeDtypeStruct(own.shape, BF16)] * 2,
        scratch_shapes=[
            pltpu.VMEM((rows, width), BF16),
            pltpu.VMEM((rows, half), BF16),
            pltpu.VMEM((width, half), BF16),
            pltpu.VMEM((half, width), BF16),
            pltpu.SemaphoreType.DMA((2 * (half // TILE),)),
        ],
        compiler_params=pltpu.CompilerParams(vmem_limit_bytes=25 * MIB),
        cost_estimate=pl.CostEstimate(
            flops=4 * rows * width * half,
            transcendentals=rows * half,
            bytes_accessed=4 * width * half + 8 * rows * width,
        ),
        name="experts",
    )(own, other, in_hbm(w_first), in_hbm(w_second))


def combine_kernel(after_out, mod, pick0, pick1, prob, *rest):
    backs, (result, after, flat, sem) = rest[: len(PAIRS)], rest[len(PAIRS) :]
    kept = pltpu.make_async_copy(after_out, after, sem)
    kept.start()
    matrix = fold_matrix(True)
    top = 0
    for back in backs:
        for j in range(back.shape[1] // 512):
            for g in range(2):
                rows = mm(matrix, back[g * 256 : (g + 1) * 256, j * 512 : (j + 1) * 512]).astype(BF16)
                for q in range(4):
                    flat[top : top + 64, q * 512 : (q + 1) * 512] = rows[q * 64 : (q + 1) * 64, :]
                top += 64
    kept.wait()
    for q in range(4):
        cut = slice(q * 512, (q + 1) * 512)
        mix = prob[:, 0:1] * mm(pick0[...], flat[:, cut]) + prob[:, 1:2] * mm(pick1[...], flat[:, cut])
        result[:, cut] = (after[:, cut] + mod[5:6, cut] * mix).astype(BF16)


def combine(after, mod, pick0, pick1, prob, backs):
    rows, width = after.shape
    vmem = pl.BlockSpec(memory_space=pltpu.VMEM)
    return pl.pallas_call(
        combine_kernel,
        in_specs=[pl.BlockSpec(memory_space=pltpu.HBM)] + [vmem] * (4 + len(backs)),
        out_specs=vmem,
        out_shape=jax.ShapeDtypeStruct((rows, width), BF16),
        scratch_shapes=[
            pltpu.VMEM((rows, width), F32),
            pltpu.VMEM((128 * sum(PAIRS), width), BF16),
            pltpu.SemaphoreType.DMA,
        ],
        compiler_params=pltpu.CompilerParams(vmem_limit_bytes=16 * MIB),
        cost_estimate=pl.CostEstimate(
            flops=3 * 10**9, transcendentals=0, bytes_accessed=7 * 10**6
        ),
        name="combine",
    )(in_hbm(after), mod, pick0, pick1, prob, *backs)


def diagonal_order(experts):
    return sorted(range(experts), key=diagonal_place)


def diagonal_place(chip):
    z, x, y = chip // 16, (chip // 4) % 4, chip % 4
    return (y - z) % 4 * 16 + (x - z) % 4 * 4 + z


def slots_of(routes, experts):
    tokens = routes.shape[0]
    routes = diagonal_place(routes)
    ids = jnp.arange(experts, dtype=jnp.int32)
    chosen = [(routes[:, k : k + 1] == ids[None, :]) for k in range(TOP)]
    taken = sum(c.astype(BF16) for c in chosen)
    order = jnp.arange(tokens, dtype=jnp.int32)
    earlier = (order[:, None] > order[None, :]).astype(BF16)
    before = mm(earlier, taken)
    slots = []
    for k in range(TOP):
        rank = jnp.sum(jnp.where(chosen[k], before, 0.0), axis=1).astype(jnp.int32)
        slots.append((rank // 2) * (2 * experts) + routes[:, k] * 2 + rank % 2)
    return slots


def body(tokens, modulation, w_query, w_key, w_value, w_out, w_in, w_back, routes, route_prob):
    tok_rows, width = tokens.shape
    mod = modulation.reshape(6, width)
    pieces = jnp.concatenate([w_query, w_key, w_value, w_out.T], axis=1)
    weights = lax.all_gather(pieces, ("grp", "dev"), axis=0, tiled=True)

    xn = (normalize(tokens.astype(F32)) * (1.0 + mod[1:2]) + mod[0:1]).astype(BF16)
    experts = lax.axis_size("dev")
    rows = experts * CAP
    slots = slots_of(routes, experts)
    ids = jnp.arange(rows, dtype=jnp.int32)
    sel = sum((ids[:, None] == s[None, :]).astype(BF16) for s in slots)
    picks = [(s[:, None] == ids[None, :]).astype(BF16) for s in slots]

    after, *sends = attention(xn, tokens, mod, sel, weights)
    swap = [(0, 1), (1, 0)]

    def shuffle(rows):
        folded = rows.reshape(experts, 8, -1)
        groups = [diagonal_order(experts)]
        return lax.all_to_all(
            folded, "dev", split_axis=0, concat_axis=0, tiled=True, axis_index_groups=groups
        ).reshape(rows.shape)

    add = lambda a, b: (a.astype(F32) + b.astype(F32)).astype(BF16)
    w_first, w_second = w_in[0], w_back[0]

    own_a, own_b = [shuffle(send) for send in sends]
    mine_a, theirs_a = expert_half(own_a, lax.ppermute(own_a, "grp", swap), w_first, w_second)
    total_a = add(mine_a, lax.ppermute(theirs_a, "grp", swap))
    own_b, total_a = lax.optimization_barrier((own_b, total_a))
    back_a = shuffle(total_a)
    other_b = lax.ppermute(own_b, "grp", swap)
    mine_b, theirs_b = expert_half(own_b, other_b, w_first, w_second)
    back_a, theirs_b = lax.optimization_barrier((back_a, theirs_b))
    total_b = add(mine_b, lax.ppermute(theirs_b, "grp", swap))
    backs = [back_a, shuffle(total_b)]
    return combine(after, mod, picks[0], picks[1], route_prob, backs)


def solution(mesh):
    in_specs = (
        P(("grp", "dev"), None),
        P(("grp", "dev"), None),
        P(("grp", "dev"), None),
        P(("grp", "dev"), None),
        P(("grp", "dev"), None),
        P(None, ("grp", "dev")),
        P("dev", None, "grp"),
        P("dev", "grp", None),
        P(("grp", "dev"), None),
        P(("grp", "dev"), None),
    )
    out_specs = P(("grp", "dev"), None)
    return jax.shard_map(body, mesh=mesh, in_specs=in_specs, out_specs=out_specs, check_vma=False)
```

```python
import jax
import jax.numpy as jnp
from jax import lax
from jax.experimental import pallas as pl
from jax.experimental.pallas import tpu as pltpu
from jax.sharding import PartitionSpec as P

HEADS = 8
HDIM = 128
TOP = 2
CAP = 10
TILE = 512
WIDE = 1024
TALL = 2048
MB = 256
BF16 = jnp.bfloat16
F32 = jnp.float32
MIB = 1024 * 1024


def mm(a, b):
    return jnp.dot(a, b, preferred_element_type=F32)


def in_hbm(array):
    return pltpu.with_memory_space_constraint(array, pltpu.HBM)


def normalize(values):
    row_mean = jnp.mean(values, axis=-1, keepdims=True)
    centered = values - row_mean
    variance = jnp.mean(centered * centered, axis=-1, keepdims=True)
    return centered * lax.rsqrt(variance + 1e-06)


def fold_matrix(transposed):
    row = lax.broadcasted_iota(jnp.int32, (256, 256), 1 if transposed else 0)
    col = lax.broadcasted_iota(jnp.int32, (256, 256), 0 if transposed else 1)
    source = ((row // 2) % 4) * 64 + (row // 8) * 2 + row % 2
    return (source == col).astype(BF16)


def fold(rows, matrix):
    stacked = jnp.concatenate([rows[:, q * 512 : (q + 1) * 512] for q in range(4)], axis=0)
    return mm(matrix, stacked).astype(BF16)


def unfold_into(target, top, folded):
    matrix = fold_matrix(True)
    for g in range(2):
        flat = mm(matrix, folded[g * 256 : (g + 1) * 256, :]).astype(BF16)
        for q in range(4):
            target[top + g * 64 : top + (g + 1) * 64, q * 512 : (q + 1) * 512] = flat[
                q * 64 : (q + 1) * 64, :
            ]


def attention_kernel(xn, tok, mod, sel, weights, after_out, send, after, mixed, held, sems):
    width, inner = xn.shape[1], mixed.shape[1]
    groups = inner // WIDE
    copies = []

    def fetch(rows, cols):
        copies.append(
            pltpu.make_async_copy(weights.at[rows, cols], held.at[rows, cols], sems.at[len(copies)])
        )
        copies[-1].start()

    for n in range(groups):
        for part in range(3):
            fetch(pl.ds(0, width), pl.ds(part * inner + n * WIDE, WIDE))
    for n in range(width // TALL):
        fetch(pl.ds(n * TALL, TALL), pl.ds(3 * inner, inner))

    for n in range(groups):
        projections = []
        for part in range(3):
            copies[3 * n + part].wait()
            first = part * inner + n * WIDE
            projections.append(mm(xn[...], held[:, first : first + WIDE]).astype(BF16))
        q, k, v = projections
        for h in range(WIDE // HDIM):
            cut = slice(h * HDIM, (h + 1) * HDIM)
            scores = lax.dot_general(
                q[:, cut], k[:, cut], (((1,), (1,)), ((), ())), preferred_element_type=F32
            ) * HDIM ** (-0.5)
            exponent = jnp.exp(scores - jnp.max(scores, axis=-1, keepdims=True))
            attn = (exponent / jnp.sum(exponent, axis=-1, keepdims=True)).astype(BF16)
            mixed[:, n * WIDE + h * HDIM : n * WIDE + (h + 1) * HDIM] = mm(attn, v[:, cut]).astype(BF16)

    for n in range(width // TALL):
        copies[3 * groups + n].wait()
        cut = slice(n * TALL, (n + 1) * TALL)
        projected = lax.dot_general(
            mixed[...], held[cut, 3 * inner :], (((1,), (1,)), ((), ())), preferred_element_type=F32
        )
        after[:, cut] = tok[:, cut].astype(F32) + mod[2:3, cut] * projected

    keep = pltpu.make_async_copy(after, after_out, sems.at[len(copies)])
    keep.start()
    normed = (normalize(after[...]) * (1.0 + mod[4:5, :]) + mod[3:4, :]).astype(BF16)
    whole = sel.shape[0] * 4 // 5
    send[:, :width] = mm(sel[:whole, :], normed).astype(BF16)
    rows = mm(sel[whole:, :], normed).astype(BF16)
    matrix = fold_matrix(False)
    for g in range(2):
        send[g * 256 : (g + 1) * 256, width:] = fold(rows[g * 64 : (g + 1) * 64, :], matrix)
    keep.wait()


def attention(xn, tok, mod, sel, weights):
    rows, width = xn.shape
    inner = HEADS * HDIM
    vmem = pl.BlockSpec(memory_space=pltpu.VMEM)
    return pl.pallas_call(
        attention_kernel,
        in_specs=[vmem] * 4 + [pl.BlockSpec(memory_space=pltpu.HBM)],
        out_specs=[pl.BlockSpec(memory_space=pltpu.HBM), vmem],
        out_shape=[
            pltpu.HBM((rows, width), F32),
            jax.ShapeDtypeStruct((sel.shape[0] * 4 // 5, width * 5 // 4), BF16),
        ],
        scratch_shapes=[
            pltpu.VMEM((rows, width), F32),
            pltpu.VMEM((rows, inner), BF16),
            pltpu.VMEM((width, 4 * inner), BF16),
            pltpu.SemaphoreType.DMA((3 * (inner // WIDE) + width // TALL + 1,)),
        ],
        compiler_params=pltpu.CompilerParams(vmem_limit_bytes=26 * MIB),
        cost_estimate=pl.CostEstimate(
            flops=7 * 10**9, transcendentals=10**6, bytes_accessed=24 * 10**6
        ),
        name="attention",
    )(xn, tok, mod, sel, in_hbm(weights))


def expert_kernel(own, other, w_first, w_second, own_out, other_out, last, hidden, first, second, sems):
    width, half = first.shape
    tiles = half // TILE
    whole = own.shape[0]

    def fetch(which, n):
        source, target = ((w_first, first), (w_second, second))[which]
        cut = pl.ds(pl.multiple_of(n * TILE, TILE), TILE)
        return pltpu.make_async_copy(
            source.at[:, cut], target.at[:, cut], sems.at[which * tiles + n]
        )

    for which in range(2):
        for n in range(tiles):
            fetch(which, n).start()

    unfold_into(last, 0, own[:, width:])
    unfold_into(last, whole // 4, other[:, width:])

    @pl.loop(0, tiles)
    def _(n):
        fetch(0, n).wait()
        cut = pl.ds(pl.multiple_of(n * TILE, TILE), TILE)
        for at, rows in enumerate((own, other, last)):
            for m in range(0, rows.shape[0], MB):
                product = mm(rows[m : m + MB, :width], first[:, cut])
                hidden[at * whole + m : at * whole + m + MB, cut] = jax.nn.gelu(
                    product, approximate=True
                ).astype(BF16)

    @pl.loop(0, tiles)
    def _(n):
        fetch(1, n).wait()
        cut = pl.ds(pl.multiple_of(n * TILE, TILE), TILE)
        for at, rows in enumerate((own_out, other_out, last)):
            for m in range(0, rows.shape[0], MB):
                rows[m : m + MB, cut] = mm(
                    hidden[at * whole + m : at * whole + m + MB, :], second[:, cut]
                ).astype(BF16)

    matrix = fold_matrix(False)
    for at, rows in enumerate((own_out, other_out)):
        for g in range(2):
            top = at * (whole // 4) + g * 64
            rows[g * 256 : (g + 1) * 256, width:] = fold(last[top : top + 64, :], matrix)


def expert_half(own, other, w_first, w_second):
    width, half = w_first.shape
    rows = own.shape[0] * 5 // 2
    vmem = pl.BlockSpec(memory_space=pltpu.VMEM)
    hbm = pl.BlockSpec(memory_space=pltpu.HBM)
    return pl.pallas_call(
        expert_kernel,
        in_specs=[vmem, vmem, hbm, hbm],
        out_specs=[vmem, vmem],
        out_shape=[jax.ShapeDtypeStruct(own.shape, BF16)] * 2,
        scratch_shapes=[
            pltpu.VMEM((own.shape[0] // 2, width), BF16),
            pltpu.VMEM((rows, half), BF16),
            pltpu.VMEM((width, half), BF16),
            pltpu.VMEM((half, width), BF16),
            pltpu.SemaphoreType.DMA((2 * (half // TILE),)),
        ],
        compiler_params=pltpu.CompilerParams(vmem_limit_bytes=28 * MIB),
        cost_estimate=pl.CostEstimate(
            flops=4 * rows * width * half,
            transcendentals=rows * half,
            bytes_accessed=4 * width * half + 8 * rows * width,
        ),
        name="experts",
    )(own, other, in_hbm(w_first), in_hbm(w_second))


def combine_kernel(after_out, mod, pick0, pick1, prob, back, result_out, after, last, result, sem, sems):
    kept = pltpu.make_async_copy(after_out, after, sem)
    kept.start()
    rows, width = after.shape
    whole = back.shape[0]
    unfold_into(last, 0, back[:, width:])
    copies = []
    for q in range(4):
        cut = slice(q * 512, (q + 1) * 512)
        picked = [
            mm(pick[:, :whole], back[:, cut]) + mm(pick[:, whole:], last[:, cut])
            for pick in (pick0, pick1)
        ]
        mix = prob[:, 0:1] * picked[0] + prob[:, 1:2] * picked[1]
        if q == 0:
            kept.wait()
        result[:, cut] = (after[:, cut] + mod[5:6, cut] * mix).astype(BF16)
        copies.append(pltpu.make_async_copy(result.at[:, cut], result_out.at[:, cut], sems.at[q]))
        copies[-1].start()
    for copy in copies:
        copy.wait()


def combine(after, mod, pick0, pick1, prob, back):
    rows, width = after.shape
    vmem = pl.BlockSpec(memory_space=pltpu.VMEM)
    hbm = pl.BlockSpec(memory_space=pltpu.HBM)
    return pl.pallas_call(
        combine_kernel,
        in_specs=[hbm] + [vmem] * 5,
        out_specs=hbm,
        out_shape=jax.ShapeDtypeStruct((rows, width), BF16),
        scratch_shapes=[
            pltpu.VMEM((rows, width), F32),
            pltpu.VMEM((back.shape[0] // 4, width), BF16),
            pltpu.VMEM((rows, width), BF16),
            pltpu.SemaphoreType.DMA,
            pltpu.SemaphoreType.DMA((4,)),
        ],
        compiler_params=pltpu.CompilerParams(vmem_limit_bytes=16 * MIB),
        cost_estimate=pl.CostEstimate(
            flops=3 * 10**9, transcendentals=0, bytes_accessed=7 * 10**6
        ),
        name="combine",
    )(in_hbm(after), mod, pick0, pick1, prob, back)


def diagonal_order(experts):
    return sorted(range(experts), key=diagonal_place)


def diagonal_place(chip):
    z, x, y = chip // 16, (chip // 4) % 4, chip % 4
    return (y - z) % 4 * 16 + (x - z) % 4 * 4 + z


def slots_of(routes, experts):
    tokens = routes.shape[0]
    routes = diagonal_place(routes)
    ids = jnp.arange(experts, dtype=jnp.int32)
    chosen = [(routes[:, k : k + 1] == ids[None, :]) for k in range(TOP)]
    taken = sum(c.astype(BF16) for c in chosen)
    order = jnp.arange(tokens, dtype=jnp.int32)
    earlier = (order[:, None] > order[None, :]).astype(BF16)
    before = mm(earlier, taken)
    slots = []
    for k in range(TOP):
        rank = jnp.sum(jnp.where(chosen[k], before, 0.0), axis=1).astype(jnp.int32)
        place = routes[:, k]
        slots.append(jnp.where(rank < 8, place * 8 + rank, 8 * experts + place * 2 + rank - 8))
    return slots


def body(tokens, modulation, w_query, w_key, w_value, w_out, w_in, w_back, routes, route_prob):
    tok_rows, width = tokens.shape
    mod = modulation.reshape(6, width)
    pieces = jnp.concatenate([w_query, w_key, w_value, w_out.T], axis=1)
    weights = lax.all_gather(pieces, ("grp", "dev"), axis=0, tiled=True)

    xn = (normalize(tokens.astype(F32)) * (1.0 + mod[1:2]) + mod[0:1]).astype(BF16)
    experts = lax.axis_size("dev")
    rows = experts * CAP
    slots = slots_of(routes, experts)
    ids = jnp.arange(rows, dtype=jnp.int32)
    sel = sum((ids[:, None] == s[None, :]).astype(BF16) for s in slots)
    picks = [(s[:, None] == ids[None, :]).astype(BF16) for s in slots]

    after, send = attention(xn, tokens, mod, sel, weights)
    swap = [(0, 1), (1, 0)]

    def shuffle(rows):
        folded = rows.reshape(experts, 8, -1)
        groups = [diagonal_order(experts)]
        return lax.all_to_all(
            folded, "dev", split_axis=0, concat_axis=0, tiled=True, axis_index_groups=groups
        ).reshape(rows.shape)

    add = lambda a, b: (a.astype(F32) + b.astype(F32)).astype(BF16)
    w_first, w_second = w_in[0], w_back[0]

    own = shuffle(send)
    mine, theirs = expert_half(own, lax.ppermute(own, "grp", swap), w_first, w_second)
    back = shuffle(add(mine, lax.ppermute(theirs, "grp", swap)))
    return combine(after, mod, picks[0], picks[1], route_prob, back)


def solution(mesh):
    in_specs = (
        P(("grp", "dev"), None),
        P(("grp", "dev"), None),
        P(("grp", "dev"), None),
        P(("grp", "dev"), None),
        P(("grp", "dev"), None),
        P(None, ("grp", "dev")),
        P("dev", None, "grp"),
        P("dev", "grp", None),
        P(("grp", "dev"), None),
        P(("grp", "dev"), None),
    )
    out_specs = P(("grp", "dev"), None)
    return jax.shard_map(body, mesh=mesh, in_specs=in_specs, out_specs=out_specs, check_vma=False)
```

```python
import functools

import jax
import jax.numpy as jnp
from jax import lax
from jax.experimental import pallas as pl
from jax.experimental.pallas import tpu as pltpu
from jax.sharding import PartitionSpec as P

HEADS = 8
HDIM = 128
TOP = 2
CAP = 10
TILE = 512
WIDE = 1024
MB = 640
BF16 = jnp.bfloat16
F32 = jnp.float32
MIB = 1024 * 1024


def mm(a, b):
    return jnp.dot(a, b, preferred_element_type=F32)


def in_hbm(array):
    return pltpu.with_memory_space_constraint(array, pltpu.HBM)


def normalize(values):
    row_mean = jnp.mean(values, axis=-1, keepdims=True)
    centered = values - row_mean
    variance = jnp.mean(centered * centered, axis=-1, keepdims=True)
    return centered * lax.rsqrt(variance + 1e-06)


def fold_matrix(transposed):
    row = lax.broadcasted_iota(jnp.int32, (256, 256), 1 if transposed else 0)
    col = lax.broadcasted_iota(jnp.int32, (256, 256), 0 if transposed else 1)
    source = ((row // 2) % 4) * 64 + (row // 8) * 2 + row % 2
    return (source == col).astype(BF16)


def fold(rows, matrix):
    stacked = jnp.concatenate([rows[:, q * 512 : (q + 1) * 512] for q in range(4)], axis=0)
    return mm(matrix, stacked).astype(BF16)


def unfold_into(target, top, folded):
    matrix = fold_matrix(True)
    for g in range(2):
        flat = mm(matrix, folded[g * 256 : (g + 1) * 256, :]).astype(BF16)
        for q in range(4):
            target[top + g * 64 : top + (g + 1) * 64, q * 512 : (q + 1) * 512] = flat[
                q * 64 : (q + 1) * 64, :
            ]


def attention_kernel(xn, tok, mod, sel, weights, after_out, send, after, mixed, held, sems):
    width, inner = xn.shape[1], mixed.shape[1]
    groups = inner // WIDE
    cores = weights.shape[1]
    copies = []

    def fetch(first, count):
        cut = pl.ds(first, count)
        copies.append(
            [
                pltpu.make_async_copy(
                    weights.at[:, core, :, cut], held.at[core, :, :, cut], sems.at[len(copies), core]
                )
                for core in range(cores)
            ]
        )
        for copy in copies[-1]:
            copy.start()

    def arrived(n, cut):
        for copy in copies[n]:
            copy.wait()
        return held[:, :, :, cut].reshape(width, cut.stop - cut.start)

    for n in range(groups):
        for part in range(3):
            fetch(part * inner + n * WIDE, WIDE)
    fetch(3 * inner, inner)

    for n in range(groups):
        projections = []
        for part in range(3):
            first = part * inner + n * WIDE
            block = arrived(3 * n + part, slice(first, first + WIDE))
            projections.append(mm(xn[...], block).astype(BF16))
        q, k, v = projections
        for h in range(WIDE // HDIM):
            cut = slice(h * HDIM, (h + 1) * HDIM)
            scores = lax.dot_general(
                q[:, cut], k[:, cut], (((1,), (1,)), ((), ())), preferred_element_type=F32
            ) * HDIM ** (-0.5)
            exponent = jnp.exp(scores - jnp.max(scores, axis=-1, keepdims=True))
            attn = (exponent / jnp.sum(exponent, axis=-1, keepdims=True)).astype(BF16)
            mixed[:, n * WIDE + h * HDIM : n * WIDE + (h + 1) * HDIM] = mm(attn, v[:, cut]).astype(BF16)

    projected = lax.dot_general(
        mixed[...],
        arrived(3 * groups, slice(3 * inner, 4 * inner)),
        (((1,), (1,)), ((), ())),
        preferred_element_type=F32,
    )
    after[...] = tok[...].astype(F32) + mod[2:3, :] * projected

    keep = pltpu.make_async_copy(after, after_out, sems.at[len(copies), 0])
    keep.start()
    normed = (normalize(after[...]) * (1.0 + mod[4:5, :]) + mod[3:4, :]).astype(BF16)
    whole = sel.shape[0] * 4 // 5
    send[:, :width] = mm(sel[:whole, :], normed).astype(BF16)
    rows = mm(sel[whole:, :], normed).astype(BF16)
    matrix = fold_matrix(False)
    for g in range(2):
        send[g * 256 : (g + 1) * 256, width:] = fold(rows[g * 64 : (g + 1) * 64, :], matrix)
    keep.wait()


def attention(xn, tok, mod, sel, weights):
    rows, width = xn.shape
    inner = HEADS * HDIM
    vmem = pl.BlockSpec(memory_space=pltpu.VMEM)
    return pl.pallas_call(
        attention_kernel,
        in_specs=[vmem] * 4 + [pl.BlockSpec(memory_space=pltpu.HBM)],
        out_specs=[pl.BlockSpec(memory_space=pltpu.HBM), vmem],
        out_shape=[
            pltpu.HBM((rows, width), F32),
            jax.ShapeDtypeStruct((sel.shape[0] * 4 // 5, width * 5 // 4), BF16),
        ],
        scratch_shapes=[
            pltpu.VMEM((rows, width), F32),
            pltpu.VMEM((rows, inner), BF16),
            pltpu.VMEM((weights.shape[1], weights.shape[0], *weights.shape[2:]), BF16),
            pltpu.SemaphoreType.DMA((3 * (inner // WIDE) + 2, weights.shape[1])),
        ],
        compiler_params=pltpu.CompilerParams(vmem_limit_bytes=26 * MIB),
        cost_estimate=pl.CostEstimate(
            flops=7 * 10**9, transcendentals=10**6, bytes_accessed=24 * 10**6
        ),
        name="attention",
    )(xn, tok, mod, sel, in_hbm(weights))


def experts_kernel(has_first, has_second, *refs):
    refs = list(refs)
    source = refs.pop(0)
    weights = [refs.pop(0) for _ in range(has_first + has_second)]
    out = refs.pop(0)
    held = [refs.pop(0) for _ in weights]
    x, hidden, sems = refs
    width = x.shape[1]
    whole = x.shape[0] * 4 // 5
    tiles = width // TILE

    def fetch(which, n):
        cut = pl.ds(pl.multiple_of(n * TILE, TILE), TILE)
        return pltpu.make_async_copy(
            weights[which].at[:, cut], held[which].at[:, cut], sems.at[which, n]
        )

    for which in range(len(weights)):
        for n in range(tiles):
            fetch(which, n).start()

    if has_first:
        x[:whole, :] = source[:, :width]
        unfold_into(x, whole, source[:, width:])
        target = hidden if has_second else out

        @pl.loop(0, tiles)
        def _(n):
            fetch(0, n).wait()
            cut = pl.ds(pl.multiple_of(n * TILE, TILE), TILE)
            for m in range(0, x.shape[0], MB):
                product = mm(x[m : m + MB, :], held[0][:, cut])
                target[m : m + MB, cut] = jax.nn.gelu(product, approximate=True).astype(BF16)

    if has_second:
        inner = hidden if has_first else source

        @pl.loop(0, tiles)
        def _(n):
            fetch(len(weights) - 1, n).wait()
            cut = pl.ds(pl.multiple_of(n * TILE, TILE), TILE)
            for m in range(0, x.shape[0], MB):
                product = mm(inner[m : m + MB, :], held[-1][:, cut]).astype(BF16)
                direct = min(max(whole - m, 0), MB)
                if direct:
                    out[m : m + direct, cut] = product[:direct]
                if direct < MB:
                    x[m + direct : m + MB, cut] = product[direct:]

        matrix = fold_matrix(False)
        for g in range(2):
            top = whole + g * 64
            out[g * 256 : (g + 1) * 256, width:] = fold(x[top : top + 64, :], matrix)


def expert_rows(source, rows, w_first=None, w_second=None):
    weights = [in_hbm(w) for w in (w_first, w_second) if w is not None]
    has_first, has_second = w_first is not None, w_second is not None
    half, width = weights[0].shape
    vmem = pl.BlockSpec(memory_space=pltpu.VMEM)
    hbm = pl.BlockSpec(memory_space=pltpu.HBM)
    shape = (rows * 4 // 5, width * 5 // 4) if has_second else (rows, half)
    return pl.pallas_call(
        functools.partial(experts_kernel, has_first, has_second),
        in_specs=[vmem] + [hbm] * len(weights),
        out_specs=vmem,
        out_shape=jax.ShapeDtypeStruct(shape, BF16),
        scratch_shapes=[pltpu.VMEM(w.shape, BF16) for w in weights]
        + [
            pltpu.VMEM((rows, width), BF16),
            pltpu.VMEM((rows, half) if has_first and has_second else (8, 128), BF16),
            pltpu.SemaphoreType.DMA((len(weights), width // TILE)),
        ],
        compiler_params=pltpu.CompilerParams(vmem_limit_bytes=(10 + 9 * len(weights)) * MIB),
        cost_estimate=pl.CostEstimate(
            flops=2 * rows * width * half * len(weights),
            transcendentals=rows * half if has_first else 0,
            bytes_accessed=2 * width * half * len(weights) + 4 * rows * width,
        ),
        name="experts",
    )(source, *weights)


def combine_kernel(after_out, mod, pick0, pick1, prob, back, result_out, after, last, result, sem, sems):
    kept = pltpu.make_async_copy(after_out, after, sem)
    kept.start()
    rows, width = after.shape
    whole = back.shape[0]
    unfold_into(last, 0, back[:, width:])
    copies = []
    for q in range(4):
        cut = slice(q * 512, (q + 1) * 512)
        picked = [
            mm(pick[:, :whole], back[:, cut]) + mm(pick[:, whole:], last[:, cut])
            for pick in (pick0, pick1)
        ]
        mix = prob[:, 0:1] * picked[0] + prob[:, 1:2] * picked[1]
        if q == 0:
            kept.wait()
        result[:, cut] = (after[:, cut] + mod[5:6, cut] * mix).astype(BF16)
        copies.append(pltpu.make_async_copy(result.at[:, cut], result_out.at[:, cut], sems.at[q]))
        copies[-1].start()
    for copy in copies:
        copy.wait()


def combine(after, mod, pick0, pick1, prob, back):
    rows, width = after.shape
    vmem = pl.BlockSpec(memory_space=pltpu.VMEM)
    hbm = pl.BlockSpec(memory_space=pltpu.HBM)
    return pl.pallas_call(
        combine_kernel,
        in_specs=[hbm] + [vmem] * 5,
        out_specs=hbm,
        out_shape=jax.ShapeDtypeStruct((rows, width), BF16),
        scratch_shapes=[
            pltpu.VMEM((rows, width), F32),
            pltpu.VMEM((back.shape[0] // 4, width), BF16),
            pltpu.VMEM((rows, width), BF16),
            pltpu.SemaphoreType.DMA,
            pltpu.SemaphoreType.DMA((4,)),
        ],
        compiler_params=pltpu.CompilerParams(vmem_limit_bytes=16 * MIB),
        cost_estimate=pl.CostEstimate(
            flops=3 * 10**9, transcendentals=0, bytes_accessed=7 * 10**6
        ),
        name="combine",
    )(in_hbm(after), mod, pick0, pick1, prob, back)


def diagonal_order(experts):
    return sorted(range(experts), key=diagonal_place)


def diagonal_place(chip):
    z, x, y = chip // 16, (chip // 4) % 4, chip % 4
    return (y - z) % 4 * 16 + (x - z) % 4 * 4 + z


def slots_of(routes, experts):
    tokens = routes.shape[0]
    routes = diagonal_place(routes)
    ids = jnp.arange(experts, dtype=jnp.int32)
    chosen = [(routes[:, k : k + 1] == ids[None, :]) for k in range(TOP)]
    taken = sum(c.astype(BF16) for c in chosen)
    order = jnp.arange(tokens, dtype=jnp.int32)
    earlier = (order[:, None] > order[None, :]).astype(BF16)
    before = mm(earlier, taken)
    slots = []
    for k in range(TOP):
        rank = jnp.sum(jnp.where(chosen[k], before, 0.0), axis=1).astype(jnp.int32)
        place = routes[:, k]
        slots.append(jnp.where(rank < 8, place * 8 + rank, 8 * experts + place * 2 + rank - 8))
    return slots


def body(tokens, modulation, w_query, w_key, w_value, w_out, w_in, w_back, routes, route_prob):
    tok_rows, width = tokens.shape
    mod = modulation.reshape(6, width)
    pieces = jnp.concatenate([w_query, w_key, w_value, w_out.T], axis=1)
    weights = lax.all_gather(pieces, ("dev", "grp"), axis=0, tiled=True)
    weights = weights.reshape(lax.axis_size("dev"), lax.axis_size("grp"), *pieces.shape)

    xn = (normalize(tokens.astype(F32)) * (1.0 + mod[1:2]) + mod[0:1]).astype(BF16)
    experts = lax.axis_size("dev")
    rows = experts * CAP
    slots = slots_of(routes, experts)
    ids = jnp.arange(rows, dtype=jnp.int32)
    sel = sum((ids[:, None] == s[None, :]).astype(BF16) for s in slots)
    picks = [(s[:, None] == ids[None, :]).astype(BF16) for s in slots]

    after, send = attention(xn, tokens, mod, sel, weights)
    swap = [(0, 1), (1, 0)]

    def shuffle(rows):
        folded = rows.reshape(experts, 8, -1)
        groups = [diagonal_order(experts)]
        return lax.all_to_all(
            folded, "dev", split_axis=0, concat_axis=0, tiled=True, axis_index_groups=groups
        ).reshape(rows.shape)

    add = lambda a, b: (a.astype(F32) + b.astype(F32)).astype(BF16)
    w_first, w_second = w_in[0], w_back[0]

    own = shuffle(send)
    other = lax.ppermute(own, "grp", swap)
    hidden = expert_rows(own, rows, w_first=w_first)
    other, hidden = lax.optimization_barrier((other, hidden))
    theirs = expert_rows(other, rows, w_first=w_first, w_second=w_second)
    hidden, theirs = lax.optimization_barrier((hidden, theirs))
    arrived = lax.ppermute(theirs, "grp", swap)
    mine = expert_rows(hidden, rows, w_second=w_second)
    back = shuffle(add(mine, arrived))
    return combine(after, mod, picks[0], picks[1], route_prob, back)


def solution(mesh):
    in_specs = (
        P(("grp", "dev"), None),
        P(("grp", "dev"), None),
        P(("grp", "dev"), None),
        P(("grp", "dev"), None),
        P(("grp", "dev"), None),
        P(None, ("grp", "dev")),
        P("dev", None, "grp"),
        P("dev", "grp", None),
        P(("grp", "dev"), None),
        P(("grp", "dev"), None),
    )
    out_specs = P(("grp", "dev"), None)
    return jax.shard_map(body, mesh=mesh, in_specs=in_specs, out_specs=out_specs, check_vma=False)
```

```python
import functools

import jax
import jax.numpy as jnp
from jax import lax
from jax.experimental import pallas as pl
from jax.experimental.pallas import tpu as pltpu
from jax.sharding import PartitionSpec as P

HEADS = 8
HDIM = 128
TOP = 2
CAP = 10
TILE = 512
WIDE = 1024
MB = 640
BF16 = jnp.bfloat16
F32 = jnp.float32
MIB = 1024 * 1024


def mm(a, b):
    return jnp.dot(a, b, preferred_element_type=F32)


def in_hbm(array):
    return pltpu.with_memory_space_constraint(array, pltpu.HBM)


def normalize(values):
    row_mean = jnp.mean(values, axis=-1, keepdims=True)
    centered = values - row_mean
    variance = jnp.mean(centered * centered, axis=-1, keepdims=True)
    return centered * lax.rsqrt(variance + 1e-06)


def fold_matrix(transposed):
    row = lax.broadcasted_iota(jnp.int32, (256, 256), 1 if transposed else 0)
    col = lax.broadcasted_iota(jnp.int32, (256, 256), 0 if transposed else 1)
    source = ((row // 2) % 4) * 64 + (row // 8) * 2 + row % 2
    return (source == col).astype(BF16)


def fold(rows, matrix):
    stacked = jnp.concatenate([rows[:, q * 512 : (q + 1) * 512] for q in range(4)], axis=0)
    return mm(matrix, stacked).astype(BF16)


def unfold_into(target, top, folded):
    matrix = fold_matrix(True)
    for g in range(2):
        flat = mm(matrix, folded[g * 256 : (g + 1) * 256, :]).astype(BF16)
        for q in range(4):
            target[top + g * 64 : top + (g + 1) * 64, q * 512 : (q + 1) * 512] = flat[
                q * 64 : (q + 1) * 64, :
            ]


def attention_kernel(xn, tok, mod, sel, weights, after_out, send, after, mixed, held, sems):
    width, inner = xn.shape[1], mixed.shape[1]
    groups = inner // WIDE
    cores = weights.shape[1]
    copies = []

    def fetch(first, count):
        cut = pl.ds(first, count)
        copies.append(
            [
                pltpu.make_async_copy(
                    weights.at[:, core, :, cut], held.at[core, :, :, cut], sems.at[len(copies), core]
                )
                for core in range(cores)
            ]
        )
        for copy in copies[-1]:
            copy.start()

    def arrived(n, cut):
        for copy in copies[n]:
            copy.wait()
        return held[:, :, :, cut].reshape(width, cut.stop - cut.start)

    for n in range(groups):
        for part in range(3):
            fetch(part * inner + n * WIDE, WIDE)
    fetch(3 * inner, inner)

    for n in range(groups):
        projections = []
        for part in range(3):
            first = part * inner + n * WIDE
            block = arrived(3 * n + part, slice(first, first + WIDE))
            projections.append(mm(xn[...], block).astype(BF16))
        q, k, v = projections
        for h in range(WIDE // HDIM):
            cut = slice(h * HDIM, (h + 1) * HDIM)
            scores = lax.dot_general(
                q[:, cut], k[:, cut], (((1,), (1,)), ((), ())), preferred_element_type=F32
            ) * HDIM ** (-0.5)
            exponent = jnp.exp(scores - jnp.max(scores, axis=-1, keepdims=True))
            attn = (exponent / jnp.sum(exponent, axis=-1, keepdims=True)).astype(BF16)
            mixed[:, n * WIDE + h * HDIM : n * WIDE + (h + 1) * HDIM] = mm(attn, v[:, cut]).astype(BF16)

    projected = lax.dot_general(
        mixed[...],
        arrived(3 * groups, slice(3 * inner, 4 * inner)),
        (((1,), (1,)), ((), ())),
        preferred_element_type=F32,
    )
    after[...] = tok[...].astype(F32) + mod[2:3, :] * projected

    keep = pltpu.make_async_copy(after, after_out, sems.at[len(copies), 0])
    keep.start()
    normed = (normalize(after[...]) * (1.0 + mod[4:5, :]) + mod[3:4, :]).astype(BF16)
    whole = sel.shape[0] * 4 // 5
    send[:, :width] = mm(sel[:whole, :], normed).astype(BF16)
    rows = mm(sel[whole:, :], normed).astype(BF16)
    matrix = fold_matrix(False)
    for g in range(2):
        send[g * 256 : (g + 1) * 256, width:] = fold(rows[g * 64 : (g + 1) * 64, :], matrix)
    keep.wait()


def attention(xn, tok, mod, sel, weights):
    rows, width = xn.shape
    inner = HEADS * HDIM
    vmem = pl.BlockSpec(memory_space=pltpu.VMEM)
    return pl.pallas_call(
        attention_kernel,
        in_specs=[vmem] * 4 + [pl.BlockSpec(memory_space=pltpu.HBM)],
        out_specs=[pl.BlockSpec(memory_space=pltpu.HBM), vmem],
        out_shape=[
            pltpu.HBM((rows, width), F32),
            jax.ShapeDtypeStruct((sel.shape[0] * 4 // 5, width * 5 // 4), BF16),
        ],
        scratch_shapes=[
            pltpu.VMEM((rows, width), F32),
            pltpu.VMEM((rows, inner), BF16),
            pltpu.VMEM((weights.shape[1], weights.shape[0], *weights.shape[2:]), BF16),
            pltpu.SemaphoreType.DMA((3 * (inner // WIDE) + 2, weights.shape[1])),
        ],
        compiler_params=pltpu.CompilerParams(vmem_limit_bytes=26 * MIB),
        cost_estimate=pl.CostEstimate(
            flops=7 * 10**9, transcendentals=10**6, bytes_accessed=24 * 10**6
        ),
        name="attention",
    )(xn, tok, mod, sel, in_hbm(weights))


def experts_kernel(has_first, has_second, *refs):
    refs = list(refs)
    source = refs.pop(0)
    weights = [refs.pop(0) for _ in range(has_first + has_second)]
    out = refs.pop(0)
    held = [refs.pop(0) for _ in weights]
    x, hidden, sems = refs
    width = x.shape[1]
    whole = x.shape[0] * 4 // 5
    tiles = width // TILE

    def fetch(which, n):
        cut = pl.ds(pl.multiple_of(n * TILE, TILE), TILE)
        return pltpu.make_async_copy(
            weights[which].at[:, cut], held[which].at[:, cut], sems.at[which, n]
        )

    for which in range(len(weights)):
        for n in range(tiles):
            fetch(which, n).start()

    if has_first:
        x[:whole, :] = source[:, :width]
        unfold_into(x, whole, source[:, width:])
        target = hidden if has_second else out

        @pl.loop(0, tiles)
        def _(n):
            fetch(0, n).wait()
            cut = pl.ds(pl.multiple_of(n * TILE, TILE), TILE)
            for m in range(0, x.shape[0], MB):
                product = mm(x[m : m + MB, :], held[0][:, cut])
                target[m : m + MB, cut] = jax.nn.gelu(product, approximate=True).astype(BF16)

    if has_second:
        inner = hidden if has_first else source

        @pl.loop(0, tiles)
        def _(n):
            fetch(len(weights) - 1, n).wait()
            cut = pl.ds(pl.multiple_of(n * TILE, TILE), TILE)
            for m in range(0, x.shape[0], MB):
                product = mm(inner[m : m + MB, :], held[-1][:, cut]).astype(BF16)
                direct = min(max(whole - m, 0), MB)
                if direct:
                    out[m : m + direct, cut] = product[:direct]
                if direct < MB:
                    x[m + direct : m + MB, cut] = product[direct:]

        matrix = fold_matrix(False)
        for g in range(2):
            top = whole + g * 64
            out[g * 256 : (g + 1) * 256, width:] = fold(x[top : top + 64, :], matrix)


def expert_rows(source, rows, w_first=None, w_second=None):
    weights = [in_hbm(w) for w in (w_first, w_second) if w is not None]
    has_first, has_second = w_first is not None, w_second is not None
    half, width = weights[0].shape
    vmem = pl.BlockSpec(memory_space=pltpu.VMEM)
    hbm = pl.BlockSpec(memory_space=pltpu.HBM)
    shape = (rows * 4 // 5, width * 5 // 4) if has_second else (rows, half)
    return pl.pallas_call(
        functools.partial(experts_kernel, has_first, has_second),
        in_specs=[vmem] + [hbm] * len(weights),
        out_specs=vmem,
        out_shape=jax.ShapeDtypeStruct(shape, BF16),
        scratch_shapes=[pltpu.VMEM(w.shape, BF16) for w in weights]
        + [
            pltpu.VMEM((rows, width), BF16),
            pltpu.VMEM((rows, half) if has_first and has_second else (8, 128), BF16),
            pltpu.SemaphoreType.DMA((len(weights), width // TILE)),
        ],
        compiler_params=pltpu.CompilerParams(vmem_limit_bytes=(10 + 9 * len(weights)) * MIB),
        cost_estimate=pl.CostEstimate(
            flops=2 * rows * width * half * len(weights),
            transcendentals=rows * half if has_first else 0,
            bytes_accessed=2 * width * half * len(weights) + 4 * rows * width,
        ),
        name="experts",
    )(source, *weights)


def add_kernel(a, b, total):
    total[...] = (a[...].astype(F32) + b[...].astype(F32)).astype(BF16)


def add_rows(a, b):
    vmem = pl.BlockSpec(memory_space=pltpu.VMEM)
    return pl.pallas_call(
        add_kernel,
        in_specs=[vmem] * 2,
        out_specs=vmem,
        out_shape=jax.ShapeDtypeStruct(a.shape, BF16),
        compiler_params=pltpu.CompilerParams(vmem_limit_bytes=4 * MIB),
        cost_estimate=pl.CostEstimate(
            flops=a.size, transcendentals=0, bytes_accessed=6 * a.size
        ),
        name="add",
    )(a, b)


def combine_kernel(after_out, mod, pick0, pick1, prob, back, result_out, after, last, result, sem, sems):
    kept = pltpu.make_async_copy(after_out, after, sem)
    kept.start()
    rows, width = after.shape
    whole = back.shape[0]
    unfold_into(last, 0, back[:, width:])
    copies = []
    for q in range(4):
        cut = slice(q * 512, (q + 1) * 512)
        picked = [
            mm(pick[:, :whole], back[:, cut]) + mm(pick[:, whole:], last[:, cut])
            for pick in (pick0, pick1)
        ]
        mix = prob[:, 0:1] * picked[0] + prob[:, 1:2] * picked[1]
        if q == 0:
            kept.wait()
        result[:, cut] = (after[:, cut] + mod[5:6, cut] * mix).astype(BF16)
        copies.append(pltpu.make_async_copy(result.at[:, cut], result_out.at[:, cut], sems.at[q]))
        copies[-1].start()
    for copy in copies:
        copy.wait()


def combine(after, mod, pick0, pick1, prob, back):
    rows, width = after.shape
    vmem = pl.BlockSpec(memory_space=pltpu.VMEM)
    hbm = pl.BlockSpec(memory_space=pltpu.HBM)
    return pl.pallas_call(
        combine_kernel,
        in_specs=[hbm] + [vmem] * 5,
        out_specs=hbm,
        out_shape=jax.ShapeDtypeStruct((rows, width), BF16),
        scratch_shapes=[
            pltpu.VMEM((rows, width), F32),
            pltpu.VMEM((back.shape[0] // 4, width), BF16),
            pltpu.VMEM((rows, width), BF16),
            pltpu.SemaphoreType.DMA,
            pltpu.SemaphoreType.DMA((4,)),
        ],
        compiler_params=pltpu.CompilerParams(vmem_limit_bytes=16 * MIB),
        cost_estimate=pl.CostEstimate(
            flops=3 * 10**9, transcendentals=0, bytes_accessed=7 * 10**6
        ),
        name="combine",
    )(in_hbm(after), mod, pick0, pick1, prob, back)


def diagonal_order(experts):
    return sorted(range(experts), key=diagonal_place)


def diagonal_place(chip):
    z, x, y = chip // 16, (chip // 4) % 4, chip % 4
    return (y - z) % 4 * 16 + (x - z) % 4 * 4 + z


def slots_of(routes, experts):
    tokens = routes.shape[0]
    routes = diagonal_place(routes)
    ids = jnp.arange(experts, dtype=jnp.int32)
    chosen = [(routes[:, k : k + 1] == ids[None, :]) for k in range(TOP)]
    taken = sum(c.astype(BF16) for c in chosen)
    order = jnp.arange(tokens, dtype=jnp.int32)
    earlier = (order[:, None] > order[None, :]).astype(BF16)
    before = mm(earlier, taken)
    slots = []
    for k in range(TOP):
        rank = jnp.sum(jnp.where(chosen[k], before, 0.0), axis=1).astype(jnp.int32)
        place = routes[:, k]
        slots.append(jnp.where(rank < 8, place * 8 + rank, 8 * experts + place * 2 + rank - 8))
    return slots


def body(tokens, modulation, w_query, w_key, w_value, w_out, w_in, w_back, routes, route_prob):
    tok_rows, width = tokens.shape
    mod = modulation.reshape(6, width)
    pieces = jnp.concatenate([w_query, w_key, w_value, w_out.T], axis=1)
    weights = lax.all_gather(pieces, ("dev", "grp"), axis=0, tiled=True)
    weights = weights.reshape(lax.axis_size("dev"), lax.axis_size("grp"), *pieces.shape)

    xn = (normalize(tokens.astype(F32)) * (1.0 + mod[1:2]) + mod[0:1]).astype(BF16)
    experts = lax.axis_size("dev")
    rows = experts * CAP
    slots = slots_of(routes, experts)
    ids = jnp.arange(rows, dtype=jnp.int32)
    sel = sum((ids[:, None] == s[None, :]).astype(BF16) for s in slots)
    picks = [(s[:, None] == ids[None, :]).astype(BF16) for s in slots]

    after, send = attention(xn, tokens, mod, sel, weights)
    swap = [(0, 1), (1, 0)]

    def shuffle(rows):
        folded = rows.reshape(experts, 8, -1)
        groups = [diagonal_order(experts)]
        return lax.all_to_all(
            folded, "dev", split_axis=0, concat_axis=0, tiled=True, axis_index_groups=groups
        ).reshape(rows.shape)

    w_first, w_second = w_in[0], w_back[0]

    own = shuffle(send)
    other = lax.ppermute(own, "grp", swap)
    hidden = expert_rows(own, rows, w_first=w_first)
    other, hidden = lax.optimization_barrier((other, hidden))
    theirs = expert_rows(other, rows, w_first=w_first, w_second=w_second)
    hidden, theirs = lax.optimization_barrier((hidden, theirs))
    arrived = lax.ppermute(theirs, "grp", swap)
    mine = expert_rows(hidden, rows, w_second=w_second)
    back = shuffle(add_rows(mine, arrived))
    return combine(after, mod, picks[0], picks[1], route_prob, back)


def solution(mesh):
    in_specs = (
        P(("grp", "dev"), None),
        P(("grp", "dev"), None),
        P(("grp", "dev"), None),
        P(("grp", "dev"), None),
        P(("grp", "dev"), None),
        P(None, ("grp", "dev")),
        P("dev", None, "grp"),
        P("dev", "grp", None),
        P(("grp", "dev"), None),
        P(("grp", "dev"), None),
    )
    out_specs = P(("grp", "dev"), None)
    return jax.shard_map(body, mesh=mesh, in_specs=in_specs, out_specs=out_specs, check_vma=False)
```
